32 devices in a mesh: parts: 2 (over x), blk: 16 (over z, y, core).
Axes of the slice: x: 2, y: 2, z: 4, core: 2. Of those that a mesh axis runs over, the one named last changes fastest.
Arguments:
- queries: bfloat16 [2048, 4096], P(('parts', 'blk')), parts along dimension 0, may hold values from -12 to 12
- keys: bfloat16 [2048, 512], P(('parts', 'blk')), parts along dimension 0, may hold values from -12 to 12
- values: bfloat16 [2048, 512], P(('parts', 'blk')), parts along dimension 0, may hold values from -6 to 6
- span_order: int32 [64], P('parts'), parts along dimension 0, may hold values from 0 to 31, as said below
Outputs:
- attended: bfloat16 [2048, 4096], P(('parts', 'blk')), parts along dimension 0
The draws below stay inside these ranges and needn't reach their ends.
There are 2 independent parts, one for each index of `parts`. The reference program is written for one: setup_inputs(seed, part) draws one part's arguments, and reference() takes and returns one part's arrays. A program takes and returns all parts, laid end to end along the dimension named above; each array names one. Nothing has to cross between parts.
Inputs may be any that keep to these rules, and one draw needn't show every extreme that they name: `span_order`: a permutation of the 32 blocks; slots 2i and 2i+1 hold blocks c and 31 - c for some c.
All inputs are finite; a program needn't handle non-finite values.
Results may differ from the reference program's by a relative error of at most 0.0065.
Values may be sent and summed in bfloat16 or wider, within the bound.
A program may use at most 64 MiB of HBM per device.

```python
import jax
import jax.numpy as jnp
from jax import lax

HEADS = 32
KV_HEADS = 4
HEAD = 128
TOK_DEV = 64
SPANS = 32
TOKENS = 1024


def draw_queries(key, part):
    base = jax.random.normal(jax.random.fold_in(key, 13), (TOKENS, HEADS * HEAD), jnp.float32)
    return jnp.clip(base, -6.0, 6.0).astype(jnp.bfloat16)


def draw_keys(key, part):
    base = jax.random.normal(jax.random.fold_in(key, 23), (TOKENS, KV_HEADS * HEAD), jnp.float32)
    return jnp.clip(base, -6.0, 6.0).astype(jnp.bfloat16)


def draw_span_order(key, part):
    pairs = SPANS // 2
    owner = jax.random.permutation(jax.random.fold_in(key, 31), pairs)
    flips = jax.random.randint(jax.random.fold_in(key, 32), (pairs,), 0, 2)
    lower = owner
    upper = SPANS - 1 - owner
    first = jnp.where(flips == 1, upper, lower)
    second = jnp.where(flips == 1, lower, upper)
    return jnp.stack([first, second], axis=1).reshape(SPANS).astype(jnp.int32)


def steps_of(stream_key, extent, pieces, low, high):
    def one(axis_at, shards_of):
        draws = jax.random.uniform(jax.random.fold_in(jax.random.fold_in(stream_key, 6), axis_at), (shards_of,), jnp.float32, low / len(pieces), high / len(pieces))
        return jnp.repeat(jnp.exp(draws), extent[axis_at] // shards_of).reshape((-1,) + (1,) * (len(extent) - axis_at - 1))

    factor_of = one(*pieces[0])
    for cut in pieces[1:]:
        factor_of = factor_of * one(*cut)
    return factor_of


def noise(own_key, extent, width, limit, cuts=(), held_as=jnp.bfloat16):
    level = steps_of(own_key, extent, cuts, -0.22, 0.18) if cuts else 1.0
    values = jax.random.normal(own_key, extent, jnp.float32) * width * level
    return jnp.minimum(jnp.maximum(values, -limit), limit).astype(held_as)


def setup_inputs(seed: int = 0, part: int = 0) -> dict:
    key_list = jax.random.split(jax.random.key(seed), 5)
    own_keys = jax.random.split(jax.random.fold_in(key_list[4], part), 5)
    queries = draw_queries(jax.random.fold_in(jax.random.fold_in(key_list[4], part), 71), part)
    keys = draw_keys(jax.random.fold_in(jax.random.fold_in(key_list[4], part), 71), part)
    values = noise(own_keys[2], (TOKENS, KV_HEADS * HEAD), 1.0, 6.0, ((0, 16),))
    span_order = draw_span_order(jax.random.fold_in(jax.random.fold_in(key_list[4], part), 71), part)
    return dict(queries=queries, keys=keys, values=values, span_order=span_order)


def reference(queries, keys, values, span_order):
    span = TOK_DEV // 2
    group = HEADS // KV_HEADS
    rows = jnp.arange(TOKENS, dtype=jnp.int32)
    position = (span_order[rows // span] * span + rows % span).astype(jnp.int32)
    qall = queries.astype(jnp.float32).reshape(TOKENS, KV_HEADS, group, HEAD)
    kall = keys.astype(jnp.float32).reshape(TOKENS, KV_HEADS, HEAD)
    vall = values.astype(jnp.float32).reshape(TOKENS, KV_HEADS, HEAD)
    scale = 1.0 / (HEAD ** 0.5)
    block = 128
    count = TOKENS // block

    def one_block(index):
        start = (index * block).astype(jnp.int32)
        qblock = lax.dynamic_slice_in_dim(qall, start, block, 0)
        pblock = lax.dynamic_slice_in_dim(position, start, block, 0)
        scores = jnp.einsum('rkgd,ckd->kgrc', qblock, kall) * scale
        scores = jnp.where(position[None, None, None, :] <= pblock[None, None, :, None], scores, -jnp.inf)
        top = jnp.max(scores, axis=-1, keepdims=True)
        expo = jnp.exp(scores - top)
        total = jnp.sum(expo, axis=-1)
        weights = expo.astype(jnp.bfloat16).astype(jnp.float32)
        summed = jnp.einsum('kgrc,ckd->kgrd', weights, vall) / total[..., None]
        return summed.transpose(2, 0, 1, 3).reshape(block, HEADS * HEAD).astype(jnp.bfloat16)

    result = lax.map(one_block, jnp.arange(count, dtype=jnp.int32))
    return result.reshape(TOKENS, HEADS * HEAD)
```

```python
import functools

import jax
import jax.numpy as jnp
from jax import lax
from jax.experimental import pallas as pl
from jax.experimental.pallas import tpu as pltpu
from jax.sharding import PartitionSpec as P

HEAD = 128


def from_partner(value, axis, bit):
    return lax.ppermute(value, axis, [(i, i ^ 1 << bit) for i in range(lax.axis_size(axis))])


def passed_along(value, axis, by):
    count = lax.axis_size(axis)
    return lax.ppermute(value, axis, [(i, (i + by) % count) for i in range(count)])


def attend(state, query_rows, query_pos, key_rows, value_rows, key_pos, scale):
    running, total, summed = state
    scores = (
        jnp.einsum("rkgd,ckd->kgrc", query_rows, key_rows, preferred_element_type=jnp.float32)
        * scale
    )
    scores = jnp.where(
        key_pos[None, None, None, :] <= query_pos[None, None, :, None], scores, -jnp.inf
    )
    newest = jnp.maximum(running, jnp.max(scores, axis=-1))
    factor = jnp.exp(running - newest)
    expo = jnp.exp(scores - newest[..., None])
    total = total * factor + jnp.sum(expo, axis=-1)
    weights = expo.astype(jnp.bfloat16)
    summed = summed * factor[..., None] + jnp.einsum(
        "kgrc,ckd->kgrd", weights, value_rows, preferred_element_type=jnp.float32
    )
    return (newest, total, summed)


def block_width(count, unit):
    number = count // unit
    best = 1
    for divisor in range(1, number + 1):
        if number % divisor == 0 and divisor * unit <= 1024:
            best = divisor
    return best * unit


def sweep(state, query_rows, query_pos, key_rows, value_rows, key_pos, scale, width):
    count = key_rows.shape[0]
    blocks = count // width
    stacked = (
        key_rows.reshape((blocks, width) + key_rows.shape[1:]),
        value_rows.reshape((blocks, width) + value_rows.shape[1:]),
        key_pos.reshape(blocks, width),
    )

    def step(carry, item):
        return (attend(carry, query_rows, query_pos, item[0], item[1], item[2], scale), None)

    final, unused = lax.scan(step, state, stacked)
    return final


def fresh(kv_heads, group, count):
    return (
        jnp.full((kv_heads, group, count), -1e30, jnp.float32),
        jnp.zeros((kv_heads, group, count), jnp.float32),
        jnp.zeros((kv_heads, group, count, HEAD), jnp.float32),
    )


def butterfly(data, member, width_bits, trade):
    current = data[:, None]
    for bit in range(width_bits):
        mine = member // 2**bit % 2
        shaped = current.reshape((current.shape[0] // 2, 2) + current.shape[1:])
        keep = lax.dynamic_index_in_dim(shaped, mine, 1, keepdims=False)
        send = lax.dynamic_index_in_dim(shaped, 1 - mine, 1, keepdims=False)
        got = trade(send, bit)
        lower = jnp.where(mine == 0, keep, got)
        upper = jnp.where(mine == 0, got, keep)
        joined = jnp.stack([lower, upper], axis=1)
        current = joined.reshape(
            (joined.shape[0], joined.shape[1] * joined.shape[2]) + joined.shape[3:]
        )
    return current[0]


def per_device(queries, keys, values, span_order):
    rows = queries.shape[0]
    span = rows // 2
    kv_heads = keys.shape[1] // HEAD
    group = queries.shape[1] // (kv_heads * HEAD)
    scale = 1.0 / HEAD**0.5
    width_bits = kv_heads.bit_length() - 1
    member = lax.axis_index("blk") % kv_heads
    group_index = lax.axis_index("blk") // kv_heads
    cycle = lax.axis_size("blk") // kv_heads
    group_rows = kv_heads * rows
    q_parts = queries.reshape(rows, kv_heads, group * HEAD).transpose(1, 0, 2)
    k_parts = keys.reshape(rows, kv_heads, HEAD).transpose(1, 0, 2)
    v_parts = values.reshape(rows, kv_heads, HEAD).transpose(1, 0, 2)
    packed = jnp.concatenate([q_parts, k_parts, v_parts], axis=2)

    def trade_in(item, bit):
        return from_partner(item, "blk", bit)

    regrouped = butterfly(packed, member, width_bits, trade_in).reshape(
        group_rows, group * HEAD + 2 * HEAD
    )
    q_mine = regrouped[:, : group * HEAD].reshape(group_rows, 1, group, HEAD)
    kv_buffer = regrouped[:, group * HEAD :]
    index = group_index * group_rows + jnp.arange(group_rows, dtype=jnp.int32)
    query_pos = span_order[index // span] * span + index % span
    steps = cycle.bit_length() - 1
    for level in range(steps):
        arrived = passed_along(kv_buffer, "blk", kv_heads * 2**level)
        kv_buffer = jnp.concatenate([arrived, kv_buffer], axis=0)
    count = kv_buffer.shape[0]
    index = ((group_index + 1) * group_rows + jnp.arange(count, dtype=jnp.int32)) % count
    key_pos = span_order[index // span] * span + index % span
    key_rows = kv_buffer[:, :HEAD].reshape(count, 1, HEAD)
    value_rows = kv_buffer[:, HEAD:].reshape(count, 1, HEAD)
    width = block_width(count, group_rows)
    running, total, summed = sweep(
        fresh(1, group, group_rows), q_mine, query_pos, key_rows, value_rows, key_pos, scale, width
    )
    normed = (summed / total[..., None]).astype(jnp.bfloat16)
    result_rows = normed[0].transpose(1, 0, 2).reshape(kv_heads, rows, group * HEAD)

    def trade_out(item, bit):
        return from_partner(item, "blk", bit)

    returned = butterfly(result_rows, member, width_bits, trade_out)
    return returned.transpose(1, 0, 2).reshape(rows, kv_heads * group * HEAD)


MASKED = -1e30
LOG2E = 1.4426950408889634
MESH = pl.DeviceIdType.MESH
SEMAPHORES = 512


def units_of(groups):
    far = groups // 2
    found = []
    for distance in range(1, far + 1):
        for side in (-1, 1):
            half = None if distance < far else (0 if side < 0 else 1)
            found.append((distance, side, half))
    return found


def fused_kernel(
    n, order_ref, q_hbm, k_hbm, v_hbm, out_hbm,
    kv, q_ref, bias, out_ref, local_sem, send_sem, recv_sem,
):
    rows = q_hbm.shape[0]
    span = rows // 2
    kv_heads = kv.shape[0]
    tokens = kv.shape[1]
    group = q_hbm.shape[1] // (kv_heads * HEAD)
    groups = n // 4
    me = lax.axis_index("blk")
    base = me - me % 4
    core = me % 2
    side_bit = me // 2 % 2
    sib = base + 2 * side_bit + (1 - core)
    partner = base + 2 * (1 - side_bit) + core
    cross = base + 2 * (1 - side_bit) + (1 - core)
    ring = {1: (me + 4) % n, -1: (me + n - 4) % n}
    units = units_of(groups)
    far = groups // 2

    local = []

    def local_copy(src, dst):
        copy = pltpu.make_async_copy(src, dst, local_sem.at[len(local)])
        copy.start()
        local.append(copy)
        return copy

    own_rows = pl.ds(pl.multiple_of(me * rows, rows), rows)
    fills = []
    for k in range(kv_heads):
        columns = pl.ds(k * HEAD, HEAD)
        fills.append(
            (
                local_copy(k_hbm.at[:, columns], kv.at[k, own_rows, pl.ds(0, HEAD)]),
                local_copy(v_hbm.at[:, columns], kv.at[k, own_rows, pl.ds(HEAD, HEAD)]),
            )
        )
    q_copy = local_copy(q_hbm, q_ref)

    barrier = pltpu.get_barrier_semaphore()
    for other in (sib, partner, ring[1], ring[-1]):
        pl.semaphore_signal(barrier, inc=1, device_id={"blk": other}, device_id_type=MESH)

    q_span = [order_ref[2 * me], order_ref[2 * me + 1]]
    row = lax.broadcasted_iota(jnp.int32, (rows, 128), 0)
    lane = lax.broadcasted_iota(jnp.int32, (rows, 128), 1)
    q_pos = jnp.where(row < span, q_span[0], q_span[1]) * span + row % span
    per_tile = 128 // span
    for tile in range(tokens // 128):
        held = jnp.full((rows, 128), order_ref[tile * per_tile], jnp.int32)
        for i in range(1, per_tile):
            held = jnp.where(lane >= i * span, order_ref[tile * per_tile + i], held)
        k_pos = held * span + lane % span
        bias[:, tile * 128 : (tile + 1) * 128] = jnp.where(k_pos <= q_pos, 0.0, MASKED)

    pl.semaphore_wait(barrier, 4)

    sent = []

    def piece(k, slot, half):
        if half is None:
            return kv.at[k, pl.ds(pl.multiple_of(slot * rows, rows), rows)]
        return kv.at[k, pl.ds(pl.multiple_of(slot * rows + half * span, span), span)]

    def remote(k, slot, half, to, send):
        ref = piece(k, slot, half)
        return pltpu.make_async_remote_copy(
            src_ref=ref,
            dst_ref=ref,
            send_sem=send,
            recv_sem=recv_sem.at[k, slot, half or 0],
            device_id={"blk": to},
            device_id_type=MESH,
        )

    def send(k, slot, half, to):
        copy = remote(k, slot, half, to, send_sem.at[len(sent)])
        copy.start()
        sent.append(copy)

    def arrive(k, slot, half):
        remote(k, slot, half, sib, send_sem.at[0]).wait_recv()

    def slot_at(origin, distance, side):
        return (origin + n + side * 4 * distance) % n

    def start_ring(k, origin):
        for side in (-1, 1):
            half = None if far > 1 else (0 if side < 0 else 1)
            send(k, origin, half, ring[-side])

    def own(k):
        for fill in fills[k]:
            fill.wait()
        send(k, me, None, partner)
        start_ring(k, me)
        send(k, me, None, sib)

    def along(k, origin, distance, side, half, to_partner):
        slot = slot_at(origin, distance, side)
        arrive(k, slot, half)
        if distance < far:
            ahead = None if distance + 1 < far else (0 if side < 0 else 1)
            send(k, slot, ahead, ring[-side])
        if to_partner:
            send(k, slot, half, partner)
        send(k, slot, half, sib)

    def by_partner(k):
        return k % 2 == 0

    def relay(k):
        for distance, side, half in units:
            if distance == 1:
                along(k, me, distance, side, half, by_partner(k))
        arrive(k, partner, None)
        if not by_partner(k):
            start_ring(k, partner)
        send(k, partner, None, sib)
        for distance, side, half in units:
            if distance > 1:
                along(k, me, distance, side, half, by_partner(k))
        for distance, side, half in units:
            if by_partner(k):
                slot = slot_at(partner, distance, side)
                arrive(k, slot, half)
                send(k, slot, half, sib)
            else:
                along(k, partner, distance, side, half, False)

    def gathered(k):
        for origin in (sib, cross):
            arrive(k, origin, None)
            for distance, side, half in units:
                arrive(k, slot_at(origin, distance, side), half)

    factor = LOG2E / HEAD**0.5
    stacked = min(group, 4)
    written = []

    def compute(k):
        keys = kv[k, :, :HEAD]
        values = kv[k, :, HEAD:]
        for part in range(group // stacked):
            first = k * group + part * stacked
            q = jnp.concatenate(
                [q_ref[:, (first + j) * HEAD : (first + j + 1) * HEAD] for j in range(stacked)],
                axis=0,
            )
            scores = lax.dot_general(
                q, keys, (((1,), (1,)), ((), ())), preferred_element_type=jnp.float32
            )
            scores = scores.reshape(stacked, rows, tokens) * factor + bias[...][None]
            top = jnp.max(scores, axis=-1, keepdims=True)
            expo = jnp.exp2(scores - top)
            total = jnp.sum(expo, axis=-1, keepdims=True)
            weights = expo.astype(jnp.bfloat16).reshape(stacked * rows, tokens)
            summed = jnp.dot(weights, values, preferred_element_type=jnp.float32)
            normed = (summed.reshape(stacked, rows, HEAD) / total).astype(jnp.bfloat16)
            for j in range(stacked):
                out_ref[:, (first + j) * HEAD : (first + j + 1) * HEAD] = normed[j]
        columns = pl.ds(k * group * HEAD, group * HEAD)
        written.append(local_copy(out_ref.at[:, columns], out_hbm.at[:, columns]))

    own(0)
    if kv_heads > 1:
        own(1)
    for k in range(kv_heads + 1):
        if k < kv_heads:
            relay(k)
            if k + 2 < kv_heads:
                own(k + 2)
        if k == 1:
            q_copy.wait()
        if k > 0:
            gathered(k - 1)
            compute(k - 1)
    for copy in sent:
        copy.wait_send()
    for copy in written:
        copy.wait()


def semaphores_sent(kv_heads, groups):
    count = len(units_of(groups))
    return kv_heads * (5 + 2 + 3 * count + count + 4)


def fused(n, queries, keys, values, span_order):
    rows = queries.shape[0]
    kv_heads = keys.shape[1] // HEAD
    tokens = n * rows
    anywhere = pl.BlockSpec(memory_space=pl.ANY)
    return pl.pallas_call(
        functools.partial(fused_kernel, n),
        out_shape=jax.ShapeDtypeStruct(queries.shape, jnp.bfloat16),
        in_specs=[pl.BlockSpec(memory_space=pltpu.SMEM), anywhere, anywhere, anywhere],
        out_specs=anywhere,
        scratch_shapes=[
            pltpu.VMEM((kv_heads, tokens, 2 * HEAD), jnp.bfloat16),
            pltpu.VMEM(queries.shape, jnp.bfloat16),
            pltpu.VMEM((rows, tokens), jnp.float32),
            pltpu.VMEM(queries.shape, jnp.bfloat16),
            pltpu.SemaphoreType.DMA((3 * kv_heads + 1,)),
            pltpu.SemaphoreType.DMA((semaphores_sent(kv_heads, n // 4),)),
            pltpu.SemaphoreType.DMA((kv_heads, n, 2)),
        ],
        compiler_params=pltpu.CompilerParams(collective_id=0, has_side_effects=True),
    )(span_order, queries, keys, values)


def solution(mesh):
    n = mesh.shape["blk"]

    def step(queries, keys, values, span_order):
        kv_heads = keys.shape[1] // HEAD
        needed = kv_heads * n * 2 + semaphores_sent(kv_heads, n // 4)
        if n % 8 == 0 and needed <= SEMAPHORES:
            return fused(n, queries, keys, values, span_order)
        return per_device(queries, keys, values, span_order)

    return jax.shard_map(
        step,
        mesh=mesh,
        in_specs=(
            P(("parts", "blk"), None),
            P(("parts", "blk"), None),
            P(("parts", "blk"), None),
            P("parts"),
        ),
        out_specs=P(("parts", "blk"), None),
        check_vma=False,
    )
```

```python
import functools

import jax
import jax.numpy as jnp
from jax import lax
from jax.experimental import pallas as pl
from jax.experimental.pallas import tpu as pltpu
from jax.sharding import PartitionSpec as P

HEAD = 128


def from_partner(value, axis, bit):
    return lax.ppermute(value, axis, [(i, i ^ 1 << bit) for i in range(lax.axis_size(axis))])


def passed_along(value, axis, by):
    count = lax.axis_size(axis)
    return lax.ppermute(value, axis, [(i, (i + by) % count) for i in range(count)])


def attend(state, query_rows, query_pos, key_rows, value_rows, key_pos, scale):
    running, total, summed = state
    scores = (
        jnp.einsum("rkgd,ckd->kgrc", query_rows, key_rows, preferred_element_type=jnp.float32)
        * scale
    )
    scores = jnp.where(
        key_pos[None, None, None, :] <= query_pos[None, None, :, None], scores, -jnp.inf
    )
    newest = jnp.maximum(running, jnp.max(scores, axis=-1))
    factor = jnp.exp(running - newest)
    expo = jnp.exp(scores - newest[..., None])
    total = total * factor + jnp.sum(expo, axis=-1)
    weights = expo.astype(jnp.bfloat16)
    summed = summed * factor[..., None] + jnp.einsum(
        "kgrc,ckd->kgrd", weights, value_rows, preferred_element_type=jnp.float32
    )
    return (newest, total, summed)


def block_width(count, unit):
    number = count // unit
    best = 1
    for divisor in range(1, number + 1):
        if number % divisor == 0 and divisor * unit <= 1024:
            best = divisor
    return best * unit


def sweep(state, query_rows, query_pos, key_rows, value_rows, key_pos, scale, width):
    count = key_rows.shape[0]
    blocks = count // width
    stacked = (
        key_rows.reshape((blocks, width) + key_rows.shape[1:]),
        value_rows.reshape((blocks, width) + value_rows.shape[1:]),
        key_pos.reshape(blocks, width),
    )

    def step(carry, item):
        return (attend(carry, query_rows, query_pos, item[0], item[1], item[2], scale), None)

    final, unused = lax.scan(step, state, stacked)
    return final


def fresh(kv_heads, group, count):
    return (
        jnp.full((kv_heads, group, count), -1e30, jnp.float32),
        jnp.zeros((kv_heads, group, count), jnp.float32),
        jnp.zeros((kv_heads, group, count, HEAD), jnp.float32),
    )


def butterfly(data, member, width_bits, trade):
    current = data[:, None]
    for bit in range(width_bits):
        mine = member // 2**bit % 2
        shaped = current.reshape((current.shape[0] // 2, 2) + current.shape[1:])
        keep = lax.dynamic_index_in_dim(shaped, mine, 1, keepdims=False)
        send = lax.dynamic_index_in_dim(shaped, 1 - mine, 1, keepdims=False)
        got = trade(send, bit)
        lower = jnp.where(mine == 0, keep, got)
        upper = jnp.where(mine == 0, got, keep)
        joined = jnp.stack([lower, upper], axis=1)
        current = joined.reshape(
            (joined.shape[0], joined.shape[1] * joined.shape[2]) + joined.shape[3:]
        )
    return current[0]


def per_device(queries, keys, values, span_order):
    rows = queries.shape[0]
    span = rows // 2
    kv_heads = keys.shape[1] // HEAD
    group = queries.shape[1] // (kv_heads * HEAD)
    scale = 1.0 / HEAD**0.5
    width_bits = kv_heads.bit_length() - 1
    member = lax.axis_index("blk") % kv_heads
    group_index = lax.axis_index("blk") // kv_heads
    cycle = lax.axis_size("blk") // kv_heads
    group_rows = kv_heads * rows
    q_parts = queries.reshape(rows, kv_heads, group * HEAD).transpose(1, 0, 2)
    k_parts = keys.reshape(rows, kv_heads, HEAD).transpose(1, 0, 2)
    v_parts = values.reshape(rows, kv_heads, HEAD).transpose(1, 0, 2)
    packed = jnp.concatenate([q_parts, k_parts, v_parts], axis=2)

    def trade_in(item, bit):
        return from_partner(item, "blk", bit)

    regrouped = butterfly(packed, member, width_bits, trade_in).reshape(
        group_rows, group * HEAD + 2 * HEAD
    )
    q_mine = regrouped[:, : group * HEAD].reshape(group_rows, 1, group, HEAD)
    kv_buffer = regrouped[:, group * HEAD :]
    index = group_index * group_rows + jnp.arange(group_rows, dtype=jnp.int32)
    query_pos = span_order[index // span] * span + index % span
    steps = cycle.bit_length() - 1
    for level in range(steps):
        arrived = passed_along(kv_buffer, "blk", kv_heads * 2**level)
        kv_buffer = jnp.concatenate([arrived, kv_buffer], axis=0)
    count = kv_buffer.shape[0]
    index = ((group_index + 1) * group_rows + jnp.arange(count, dtype=jnp.int32)) % count
    key_pos = span_order[index // span] * span + index % span
    key_rows = kv_buffer[:, :HEAD].reshape(count, 1, HEAD)
    value_rows = kv_buffer[:, HEAD:].reshape(count, 1, HEAD)
    width = block_width(count, group_rows)
    running, total, summed = sweep(
        fresh(1, group, group_rows), q_mine, query_pos, key_rows, value_rows, key_pos, scale, width
    )
    normed = (summed / total[..., None]).astype(jnp.bfloat16)
    result_rows = normed[0].transpose(1, 0, 2).reshape(kv_heads, rows, group * HEAD)

    def trade_out(item, bit):
        return from_partner(item, "blk", bit)

    returned = butterfly(result_rows, member, width_bits, trade_out)
    return returned.transpose(1, 0, 2).reshape(rows, kv_heads * group * HEAD)


MASKED = -1e30
LOG2E = 1.4426950408889634
MESH = pl.DeviceIdType.MESH
SEMAPHORES = 512
CHUNKS = 2


def fused_kernel(
    n, order_ref, q_hbm, k_hbm, v_hbm, out_hbm,
    kv, q_ref, bias, out_ref, local_sem, send_sem, recv_sem,
):
    rows = q_hbm.shape[0]
    span = rows // 2
    kv_heads = k_hbm.shape[1] // HEAD
    chunks = kv.shape[0]
    per_chunk = kv_heads // chunks
    tokens = kv.shape[1]
    group = q_hbm.shape[1] // (kv_heads * HEAD)
    me = lax.axis_index("blk")
    base = me - me % 4
    core = me % 2
    side_bit = me // 2 % 2
    sib = base + 2 * side_bit + (1 - core)
    partner = base + 2 * (1 - side_bit) + core
    cross = base + 2 * (1 - side_bit) + (1 - core)
    groups = n // 4
    place = me // 4
    mirrored = place * 2 // groups
    relayed = groups > 3
    edge = jnp.logical_or(place == 0, place == groups - 1)
    inner = jnp.logical_or(place == 1, place == groups - 2)
    beside_edge = (me + 4 * (1 - 2 * (1 - mirrored)) + n) % n

    def along(origin, distance):
        return (origin + 4 * (distance + mirrored * (groups - 2 * distance))) % n

    distances = list(range(1, groups))
    local = []

    def local_copy(src, dst):
        copy = pltpu.make_async_copy(src, dst, local_sem.at[len(local)])
        copy.start()
        local.append(copy)
        return copy

    own_rows = pl.ds(pl.multiple_of(me * rows, rows), rows)
    fills = []
    wide = per_chunk * HEAD
    for k in range(chunks):
        columns = pl.ds(k * wide, wide)
        fills.append(
            (
                local_copy(k_hbm.at[:, columns], kv.at[k, own_rows, pl.ds(0, wide)]),
                local_copy(v_hbm.at[:, columns], kv.at[k, own_rows, pl.ds(wide, wide)]),
            )
        )
    q_copy = local_copy(q_hbm, q_ref)

    barrier = pltpu.get_barrier_semaphore()
    others = [sib, partner] + [along(me, d) for d in distances]
    for other in others:
        pl.semaphore_signal(barrier, inc=1, device_id={"blk": other}, device_id_type=MESH)

    q_span = [order_ref[2 * me], order_ref[2 * me + 1]]
    row = lax.broadcasted_iota(jnp.int32, (rows, 128), 0)
    lane = lax.broadcasted_iota(jnp.int32, (rows, 128), 1)
    q_pos = jnp.where(row < span, q_span[0], q_span[1]) * span + row % span
    per_tile = 128 // span
    for tile in range(tokens // 128):
        held = jnp.full((rows, 128), order_ref[tile * per_tile], jnp.int32)
        for i in range(1, per_tile):
            held = jnp.where(lane >= i * span, order_ref[tile * per_tile + i], held)
        k_pos = held * span + lane % span
        bias[:, tile * 128 : (tile + 1) * 128] = jnp.where(k_pos <= q_pos, 0.0, MASKED)

    pl.semaphore_wait(barrier, len(others))

    sent = []

    def remote(k, slot, to, send):
        ref = kv.at[k, pl.ds(pl.multiple_of(slot * rows, rows), rows)]
        return pltpu.make_async_remote_copy(
            src_ref=ref,
            dst_ref=ref,
            send_sem=send,
            recv_sem=recv_sem.at[k, slot],
            device_id={"blk": to},
            device_id_type=MESH,
        )

    def send(k, slot, to, when=None):
        copy = remote(k, slot, to, send_sem.at[len(sent)])
        sent.append((copy, when))
        if when is None:
            copy.start()
        else:
            pl.when(when)(copy.start)

    def arrive(k, slot):
        remote(k, slot, sib, send_sem.at[0]).wait_recv()

    def own(k):
        for fill in fills[k]:
            fill.wait()
        for d in sorted(distances, key=lambda d: d != groups - 2):
            when = jnp.logical_not(edge) if relayed and d == groups - 1 else None
            send(k, me, along(me, d), when)
        send(k, me, sib)

    def own_across(k):
        send(k, me, partner)

    def line(k):
        for d in sorted(distances, key=lambda d: (d == groups - 1, d)):
            slot = along(me, d)
            arrive(k, slot)
            if relayed and d == groups - 2:
                send(k, slot, beside_edge, inner)
            send(k, slot, partner)
            send(k, slot, sib)

    def across(k):
        for slot in [partner] + [along(partner, d) for d in distances]:
            arrive(k, slot)
            send(k, slot, sib)

    def gathered(k):
        for origin in (sib, cross):
            for slot in [origin] + [along(origin, d) for d in distances]:
                arrive(k, slot)

    factor = LOG2E / HEAD**0.5
    stacked = min(group, 4)
    written = []

    def compute(k, part):
        at = k % per_chunk * HEAD
        keys = kv[k // per_chunk, :, at : at + HEAD]
        values = kv[k // per_chunk, :, wide + at : wide + at + HEAD]
        first = k * group + part * stacked
        q = jnp.concatenate(
            [q_ref[:, (first + j) * HEAD : (first + j + 1) * HEAD] for j in range(stacked)],
            axis=0,
        )
        scores = lax.dot_general(
            q, keys, (((1,), (1,)), ((), ())), preferred_element_type=jnp.float32
        )
        scores = scores.reshape(stacked, rows, tokens) * factor + bias[...][None]
        top = jnp.max(scores, axis=-1, keepdims=True)
        expo = jnp.exp2(scores - top)
        total = jnp.sum(expo, axis=-1, keepdims=True)
        weights = expo.astype(jnp.bfloat16).reshape(stacked * rows, tokens)
        summed = jnp.dot(weights, values, preferred_element_type=jnp.float32)
        normed = (summed.reshape(stacked, rows, HEAD) / total).astype(jnp.bfloat16)
        for j in range(stacked):
            out_ref[:, (first + j) * HEAD : (first + j + 1) * HEAD] = normed[j]
        if part == parts - 1:
            columns = pl.ds(k * group * HEAD, group * HEAD)
            written.append(local_copy(out_ref.at[:, columns], out_hbm.at[:, columns]))

    parts = group // stacked
    slots = {}
    bodies = per_chunk * parts
    for k in range(chunks):
        slots.setdefault(3 * k, []).append((line, k))
        slots.setdefault(3 * k + 4, []).append((across, k))
        slots.setdefault(3 * k + 6, []).append((gathered, k))
        for body in range(bodies):
            slots.setdefault(3 * k + 6 + 3 * body / bodies, []).append(
                (compute, k * per_chunk + body // parts, body % parts)
            )
    for k in range(chunks):
        own(k)
        if k < 2:
            own_across(k)
    q_copy.wait()
    for time in sorted(slots):
        for action in slots[time]:
            action[0](*action[1:])
            if action[0] is line and action[1] + 2 < chunks:
                own_across(action[1] + 2)
    for copy, when in sent:
        if when is None:
            copy.wait_send()
        else:
            pl.when(when)(copy.wait_send)
    for copy in written:
        copy.wait()


def semaphores_sent(kv_heads, groups):
    return kv_heads * (5 * groups + 2)


def fused(n, queries, keys, values, span_order):
    rows = queries.shape[0]
    kv_heads = keys.shape[1] // HEAD
    tokens = n * rows
    chunks = CHUNKS if kv_heads % CHUNKS == 0 else 1
    anywhere = pl.BlockSpec(memory_space=pl.ANY)
    return pl.pallas_call(
        functools.partial(fused_kernel, n),
        out_shape=jax.ShapeDtypeStruct(queries.shape, jnp.bfloat16),
        in_specs=[pl.BlockSpec(memory_space=pltpu.SMEM), anywhere, anywhere, anywhere],
        out_specs=anywhere,
        scratch_shapes=[
            pltpu.VMEM((chunks, tokens, kv_heads // chunks * 2 * HEAD), jnp.bfloat16),
            pltpu.VMEM(queries.shape, jnp.bfloat16),
            pltpu.VMEM((rows, tokens), jnp.float32),
            pltpu.VMEM(queries.shape, jnp.bfloat16),
            pltpu.SemaphoreType.DMA((3 * kv_heads + 1,)),
            pltpu.SemaphoreType.DMA((semaphores_sent(kv_heads, n // 4),)),
            pltpu.SemaphoreType.DMA((chunks, n)),
        ],
        compiler_params=pltpu.CompilerParams(collective_id=0, has_side_effects=True),
    )(span_order, queries, keys, values)


def solution(mesh):
    n = mesh.shape["blk"]

    def step(queries, keys, values, span_order):
        kv_heads = keys.shape[1] // HEAD
        needed = kv_heads * n + semaphores_sent(kv_heads, n // 4)
        if n % 8 == 0 and needed <= SEMAPHORES:
            return fused(n, queries, keys, values, span_order)
        return per_device(queries, keys, values, span_order)

    return jax.shard_map(
        step,
        mesh=mesh,
        in_specs=(
            P(("parts", "blk"), None),
            P(("parts", "blk"), None),
            P(("parts", "blk"), None),
            P("parts"),
        ),
        out_specs=P(("parts", "blk"), None),
        check_vma=False,
    )
```

```python
import functools

import jax
import jax.numpy as jnp
from jax import lax
from jax.experimental import pallas as pl
from jax.experimental.pallas import tpu as pltpu
from jax.sharding import PartitionSpec as P

HEAD = 128


def from_partner(value, axis, bit):
    return lax.ppermute(value, axis, [(i, i ^ 1 << bit) for i in range(lax.axis_size(axis))])


def passed_along(value, axis, by):
    count = lax.axis_size(axis)
    return lax.ppermute(value, axis, [(i, (i + by) % count) for i in range(count)])


def attend(state, query_rows, query_pos, key_rows, value_rows, key_pos, scale):
    running, total, summed = state
    scores = (
        jnp.einsum("rkgd,ckd->kgrc", query_rows, key_rows, preferred_element_type=jnp.float32)
        * scale
    )
    scores = jnp.where(
        key_pos[None, None, None, :] <= query_pos[None, None, :, None], scores, -jnp.inf
    )
    newest = jnp.maximum(running, jnp.max(scores, axis=-1))
    factor = jnp.exp(running - newest)
    expo = jnp.exp(scores - newest[..., None])
    total = total * factor + jnp.sum(expo, axis=-1)
    weights = expo.astype(jnp.bfloat16)
    summed = summed * factor[..., None] + jnp.einsum(
        "kgrc,ckd->kgrd", weights, value_rows, preferred_element_type=jnp.float32
    )
    return (newest, total, summed)


def block_width(count, unit):
    number = count // unit
    best = 1
    for divisor in range(1, number + 1):
        if number % divisor == 0 and divisor * unit <= 1024:
            best = divisor
    return best * unit


def sweep(state, query_rows, query_pos, key_rows, value_rows, key_pos, scale, width):
    count = key_rows.shape[0]
    blocks = count // width
    stacked = (
        key_rows.reshape((blocks, width) + key_rows.shape[1:]),
        value_rows.reshape((blocks, width) + value_rows.shape[1:]),
        key_pos.reshape(blocks, width),
    )

    def step(carry, item):
        return (attend(carry, query_rows, query_pos, item[0], item[1], item[2], scale), None)

    final, unused = lax.scan(step, state, stacked)
    return final


def fresh(kv_heads, group, count):
    return (
        jnp.full((kv_heads, group, count), -1e30, jnp.float32),
        jnp.zeros((kv_heads, group, count), jnp.float32),
        jnp.zeros((kv_heads, group, count, HEAD), jnp.float32),
    )


def butterfly(data, member, width_bits, trade):
    current = data[:, None]
    for bit in range(width_bits):
        mine = member // 2**bit % 2
        shaped = current.reshape((current.shape[0] // 2, 2) + current.shape[1:])
        keep = lax.dynamic_index_in_dim(shaped, mine, 1, keepdims=False)
        send = lax.dynamic_index_in_dim(shaped, 1 - mine, 1, keepdims=False)
        got = trade(send, bit)
        lower = jnp.where(mine == 0, keep, got)
        upper = jnp.where(mine == 0, got, keep)
        joined = jnp.stack([lower, upper], axis=1)
        current = joined.reshape(
            (joined.shape[0], joined.shape[1] * joined.shape[2]) + joined.shape[3:]
        )
    return current[0]


def per_device(queries, keys, values, span_order):
    rows = queries.shape[0]
    span = rows // 2
    kv_heads = keys.shape[1] // HEAD
    group = queries.shape[1] // (kv_heads * HEAD)
    scale = 1.0 / HEAD**0.5
    width_bits = kv_heads.bit_length() - 1
    member = lax.axis_index("blk") % kv_heads
    group_index = lax.axis_index("blk") // kv_heads
    cycle = lax.axis_size("blk") // kv_heads
    group_rows = kv_heads * rows
    q_parts = queries.reshape(rows, kv_heads, group * HEAD).transpose(1, 0, 2)
    k_parts = keys.reshape(rows, kv_heads, HEAD).transpose(1, 0, 2)
    v_parts = values.reshape(rows, kv_heads, HEAD).transpose(1, 0, 2)
    packed = jnp.concatenate([q_parts, k_parts, v_parts], axis=2)

    def trade_in(item, bit):
        return from_partner(item, "blk", bit)

    regrouped = butterfly(packed, member, width_bits, trade_in).reshape(
        group_rows, group * HEAD + 2 * HEAD
    )
    q_mine = regrouped[:, : group * HEAD].reshape(group_rows, 1, group, HEAD)
    kv_buffer = regrouped[:, group * HEAD :]
    index = group_index * group_rows + jnp.arange(group_rows, dtype=jnp.int32)
    query_pos = span_order[index // span] * span + index % span
    steps = cycle.bit_length() - 1
    for level in range(steps):
        arrived = passed_along(kv_buffer, "blk", kv_heads * 2**level)
        kv_buffer = jnp.concatenate([arrived, kv_buffer], axis=0)
    count = kv_buffer.shape[0]
    index = ((group_index + 1) * group_rows + jnp.arange(count, dtype=jnp.int32)) % count
    key_pos = span_order[index // span] * span + index % span
    key_rows = kv_buffer[:, :HEAD].reshape(count, 1, HEAD)
    value_rows = kv_buffer[:, HEAD:].reshape(count, 1, HEAD)
    width = block_width(count, group_rows)
    running, total, summed = sweep(
        fresh(1, group, group_rows), q_mine, query_pos, key_rows, value_rows, key_pos, scale, width
    )
    normed = (summed / total[..., None]).astype(jnp.bfloat16)
    result_rows = normed[0].transpose(1, 0, 2).reshape(kv_heads, rows, group * HEAD)

    def trade_out(item, bit):
        return from_partner(item, "blk", bit)

    returned = butterfly(result_rows, member, width_bits, trade_out)
    return returned.transpose(1, 0, 2).reshape(rows, kv_heads * group * HEAD)


MASKED = -1e30
LOG2E = 1.4426950408889634
MESH = pl.DeviceIdType.MESH
SEMAPHORES = 512
CHUNKS = 2
LINE = 4


def fused_kernel(
    n, order_ref, q_hbm, k_hbm, v_hbm, out_hbm,
    kv, q_ref, bias, out_ref, local_sem, send_sem, recv_sem, told,
):
    rows = q_hbm.shape[0]
    span = rows // 2
    kv_heads = k_hbm.shape[1] // HEAD
    chunks = kv.shape[0]
    per_chunk = kv_heads // chunks
    tokens = kv.shape[1]
    group = q_hbm.shape[1] // (kv_heads * HEAD)
    me = lax.axis_index("blk")
    base = me - me % 4
    core = me % 2
    side_bit = me // 2 % 2
    sib = base + 2 * side_bit + (1 - core)
    partner = base + 2 * (1 - side_bit) + core
    cross = base + 2 * (1 - side_bit) + (1 - core)
    groups = n // 4
    place = me // 4
    mirrored = place * 2 // groups
    relayed = groups > 3
    inner = jnp.logical_or(place == 1, place == groups - 2)
    beside_edge = (me + 4 * (1 - 2 * (1 - mirrored)) + n) % n

    def along(origin, distance):
        return (origin + 4 * (distance + mirrored * (groups - 2 * distance))) % n

    distances = list(range(1, groups))
    local = []

    def local_copy(src, dst):
        copy = pltpu.make_async_copy(src, dst, local_sem.at[len(local)])
        copy.start()
        local.append(copy)
        return copy

    own_rows = pl.ds(pl.multiple_of(me * rows, rows), rows)
    fills = []
    wide = per_chunk * HEAD
    for k in range(chunks):
        columns = pl.ds(k * wide, wide)
        fills.append(
            (
                local_copy(k_hbm.at[:, columns], kv.at[k, own_rows, pl.ds(0, wide)]),
                local_copy(v_hbm.at[:, columns], kv.at[k, own_rows, pl.ds(wide, wide)]),
            )
        )
    q_copy = local_copy(q_hbm, q_ref)

    barrier = pltpu.get_barrier_semaphore()
    def greet(semaphore, other):
        pl.semaphore_signal(semaphore, inc=1, device_id={"blk": other}, device_id_type=MESH)

    last = groups - 1
    for other in (sib, partner, along(me, 1)):
        greet(barrier, other)
    if relayed:
        pl.when(inner)(functools.partial(greet, barrier, along(me, last)))

    q_span = [order_ref[2 * me], order_ref[2 * me + 1]]
    row = lax.broadcasted_iota(jnp.int32, (rows, 128), 0)
    lane = lax.broadcasted_iota(jnp.int32, (rows, 128), 1)
    q_pos = jnp.where(row < span, q_span[0], q_span[1]) * span + row % span
    per_tile = 128 // span
    for tile in range(tokens // 128):
        held = jnp.full((rows, 128), order_ref[tile * per_tile], jnp.int32)
        for i in range(1, per_tile):
            held = jnp.where(lane >= i * span, order_ref[tile * per_tile + i], held)
        k_pos = held * span + lane % span
        bias[:, tile * 128 : (tile + 1) * 128] = jnp.where(k_pos <= q_pos, 0.0, MASKED)

    if relayed:

        @pl.when(inner)
        def tell():
            pl.semaphore_wait(barrier, 4)
            greet(told, along(me, 1))
            greet(told, along(me, last))

        @pl.when(jnp.logical_not(inner))
        def listen():
            pl.semaphore_wait(barrier, 3)

    else:
        pl.semaphore_wait(barrier, 3)

    sent = []

    def remote(k, slot, to, send):
        ref = kv.at[k, pl.ds(pl.multiple_of(slot * rows, rows), rows)]
        return pltpu.make_async_remote_copy(
            src_ref=ref,
            dst_ref=ref,
            send_sem=send,
            recv_sem=recv_sem.at[k, slot],
            device_id={"blk": to},
            device_id_type=MESH,
        )

    def send(k, slot, to, when=None):
        copy = remote(k, slot, to, send_sem.at[len(sent)])
        sent.append((copy, when))
        if when is None:
            copy.start()
        else:
            pl.when(when)(copy.start)

    def arrive(k, slot):
        remote(k, slot, sib, send_sem.at[0]).wait_recv()

    def own(k):
        for fill in fills[k]:
            fill.wait()
        if k == 0:
            own_across(0)
        for d in sorted(distances, key=lambda d: (d == groups - 2) == (k == 0)):
            if relayed and k == 0 and d == groups - 2:
                pl.semaphore_wait(told, 1)
            when = inner if relayed and d == last else None
            send(k, me, along(me, d), when)
        send(k, me, sib)

    def own_across(k):
        send(k, me, partner)

    def line(k):
        for d in sorted(distances, key=lambda d: (d == groups - 1, d != groups - 2, d)):
            slot = along(me, d)
            arrive(k, slot)
            if relayed and d == groups - 2:
                send(k, slot, beside_edge, inner)
            send(k, slot, partner)
            send(k, slot, sib)

    def across(k):
        for slot in [partner] + [along(partner, d) for d in distances]:
            arrive(k, slot)
            send(k, slot, sib)

    def gathered(k):
        for origin in (sib, cross):
            for slot in [origin] + [along(origin, d) for d in distances]:
                arrive(k, slot)

    factor = LOG2E / HEAD**0.5
    stacked = min(group, 4)
    written = []

    def compute(k, part):
        at = k % per_chunk * HEAD
        keys = kv[k // per_chunk, :, at : at + HEAD]
        values = kv[k // per_chunk, :, wide + at : wide + at + HEAD]
        first = k * group + part * stacked
        q = jnp.concatenate(
            [q_ref[:, (first + j) * HEAD : (first + j + 1) * HEAD] for j in range(stacked)],
            axis=0,
        )
        scores = lax.dot_general(
            q, keys, (((1,), (1,)), ((), ())), preferred_element_type=jnp.float32
        )
        scores = scores.reshape(stacked, rows, tokens) * factor + bias[...][None]
        top = jnp.max(scores, axis=-1, keepdims=True)
        expo = jnp.exp2(scores - top)
        total = jnp.sum(expo, axis=-1, keepdims=True)
        weights = expo.astype(jnp.bfloat16).reshape(stacked * rows, tokens)
        summed = jnp.dot(weights, values, preferred_element_type=jnp.float32)
        normed = (summed.reshape(stacked, rows, HEAD) / total).astype(jnp.bfloat16)
        for j in range(stacked):
            out_ref[:, (first + j) * HEAD : (first + j + 1) * HEAD] = normed[j]
        if part == parts - 1:
            columns = pl.ds(k * group * HEAD, group * HEAD)
            written.append(local_copy(out_ref.at[:, columns], out_hbm.at[:, columns]))

    parts = group // stacked
    slots = {}
    bodies = per_chunk * parts
    for k in range(chunks):
        slots.setdefault(3 * k, []).append((line, k))
        slots.setdefault(3 * k + 4, []).append((across, k))
        slots.setdefault(3 * k + 6, []).append((gathered, k))
        for body in range(bodies):
            slots.setdefault(3 * k + 6 + 3 * body / bodies, []).append(
                (compute, k * per_chunk + body // parts, body % parts)
            )
    for k in range(chunks):
        own(k)
        if k == 1:
            own_across(k)
    q_copy.wait()
    for time in sorted(slots):
        for action in slots[time]:
            action[0](*action[1:])
            if action[0] is line and action[1] + 2 < chunks:
                own_across(action[1] + 2)
    for copy, when in sent:
        if when is None:
            copy.wait_send()
        else:
            pl.when(when)(copy.wait_send)
    for copy in written:
        copy.wait()


def semaphores_sent(kv_heads, groups):
    return kv_heads * (5 * groups + 2)


def fused(n, queries, keys, values, span_order):
    rows = queries.shape[0]
    kv_heads = keys.shape[1] // HEAD
    tokens = n * rows
    chunks = CHUNKS if kv_heads % CHUNKS == 0 else 1
    anywhere = pl.BlockSpec(memory_space=pl.ANY)
    return pl.pallas_call(
        functools.partial(fused_kernel, n),
        out_shape=jax.ShapeDtypeStruct(queries.shape, jnp.bfloat16),
        in_specs=[pl.BlockSpec(memory_space=pltpu.SMEM), anywhere, anywhere, anywhere],
        out_specs=anywhere,
        scratch_shapes=[
            pltpu.VMEM((chunks, tokens, kv_heads // chunks * 2 * HEAD), jnp.bfloat16),
            pltpu.VMEM(queries.shape, jnp.bfloat16),
            pltpu.VMEM((rows, tokens), jnp.float32),
            pltpu.VMEM(queries.shape, jnp.bfloat16),
            pltpu.SemaphoreType.DMA((3 * kv_heads + 1,)),
            pltpu.SemaphoreType.DMA((semaphores_sent(kv_heads, n // 4),)),
            pltpu.SemaphoreType.DMA((chunks, n)),
            pltpu.SemaphoreType.REGULAR,
        ],
        compiler_params=pltpu.CompilerParams(collective_id=0, has_side_effects=True),
    )(span_order, queries, keys, values)


def solution(mesh):
    n = mesh.shape["blk"]

    def step(queries, keys, values, span_order):
        kv_heads = keys.shape[1] // HEAD
        needed = kv_heads * n + semaphores_sent(kv_heads, n // 4)
        if n % 8 == 0 and n // 4 <= LINE and needed <= SEMAPHORES:
            return fused(n, queries, keys, values, span_order)
        return per_device(queries, keys, values, span_order)

    return jax.shard_map(
        step,
        mesh=mesh,
        in_specs=(
            P(("parts", "blk"), None),
            P(("parts", "blk"), None),
            P(("parts", "blk"), None),
            P("parts"),
        ),
        out_specs=P(("parts", "blk"), None),
        check_vma=False,
    )
```
